32 devices in a mesh: dp: 4 (over y, x), mp: 8 (over z, core).
Axes of the slice: x: 2, y: 2, z: 4, core: 2. Of those that a mesh axis runs over, the one named last changes fastest.
Arguments:
- grad: bfloat16 [4096, 8192], P(('dp', 'mp')), as said below
- block_owner: int32 [32], replicated, may hold values from 0 to 31, as said below
- left_stat: float32 [32, 1024, 1024], P(('dp', 'mp')), as said below
- right_stat: float32 [32, 1024, 1024], P(('dp', 'mp')), as said below
- left_root: bfloat16 [32, 1024, 1024], P(('dp', 'mp'))
- right_root: bfloat16 [32, 1024, 1024], P(('dp', 'mp'))
Outputs:
- new_left: float32 [32, 1024, 1024], P(('dp', 'mp'))
- new_right: float32 [32, 1024, 1024], P(('dp', 'mp'))
- update: bfloat16 [4096, 8192], P(('dp', 'mp'))
The draws below stay inside these ranges and needn't reach their ends.
Inputs may be any that keep to these rules, and one draw needn't show every extreme that they name: `block_owner`: A permutation: each device owns exactly one block, and of each band's 8 blocks exactly 2 are owned by devices of each dp index (owner = dp index * 8 + mp index). `grad`: gradient entries, scaled per row and per column. `left_stat`: symmetric positive definite. `right_stat`: symmetric positive definite.
All inputs are finite; a program needn't handle non-finite values.
Results may differ from the reference program's by a relative error of at most 0.0039.
The reference program's roundings to bfloat16 on the way count: a program that leaves them out, or rounds other values in their place, can miss the bound.
Values may be sent and summed in bfloat16 or wider, within the bound.
No kernel may reach another device: no remote copies, remote signals or barrier semaphores. Data moves between devices by JAX's collectives and lax.ppermute only.
A program may use at most 256 MiB of HBM per device.

```python
import jax
import jax.numpy as jnp
from jax import lax

BLK = 1024
BANDS = 4
COLB = 8
GROUP = 2
NB = 32
ROWS = 4096
COLS = 8192


def draw_grad(key, part):
    key_base, key_rows, key_cols = jax.random.split(jax.random.fold_in(key, 11), 3)
    ramp = 10.0 ** (jnp.arange(ROWS, dtype=jnp.float32) / ROWS)
    row_factor = jnp.exp(jax.random.uniform(key_rows, (ROWS, 1), jnp.float32) * jnp.log(3.0))
    base = jax.random.normal(key_base, (ROWS, COLS), jnp.float32)
    col_factor = jnp.exp(jax.random.uniform(key_cols, (1, COLS), jnp.float32) * jnp.log(3.0))
    return (base * ramp[:, None] * row_factor * col_factor).astype(jnp.bfloat16)


def root_matrix(key):
    key_diag, key_off = jax.random.split(key)
    diagonal = jnp.exp(jax.random.uniform(key_diag, (NB, BLK), jnp.float32, jnp.log(0.5), jnp.log(2.0)))
    off_part = jax.random.normal(key_off, (NB, BLK, BLK), jnp.float32)
    eye = jnp.eye(BLK, dtype=jnp.float32)
    return (eye[None] * diagonal[:, :, None] + off_part * (0.5 / BLK ** 0.5)).astype(jnp.bfloat16)


def stat_block(key):
    key_mat, key_level = jax.random.split(key)
    factor_mat = jax.random.normal(key_mat, (BLK, BLK), jnp.float32)
    level = jnp.exp(jax.random.uniform(key_level, (), jnp.float32, jnp.log(0.02), jnp.log(0.3)))
    gram = jnp.dot(factor_mat, factor_mat.T, precision=lax.Precision.HIGHEST) / BLK
    return level * (gram + 0.25 * jnp.eye(BLK, dtype=jnp.float32))


def stat_matrix(key):
    return lax.map(stat_block, jax.random.split(key, NB))


def draw_left_stat(key, part):
    return stat_matrix(jax.random.fold_in(key, 41))


def draw_right_stat(key, part):
    return stat_matrix(jax.random.fold_in(key, 42))


def draw_left_root(key, part):
    return root_matrix(jax.random.fold_in(key, 21))


def draw_right_root(key, part):
    return root_matrix(jax.random.fold_in(key, 22))


def draw_block_owner(key, part):
    key_cols, key_mps = jax.random.split(jax.random.fold_in(key, 31))
    col_perm = jax.vmap(lambda k: jax.random.permutation(k, COLB))(jax.random.split(key_cols, BANDS)).astype(jnp.int32)
    mp_perm = jax.vmap(lambda k: jax.random.permutation(k, COLB))(jax.random.split(key_mps, BANDS)).astype(jnp.int32)
    ranks = jnp.arange(COLB, dtype=jnp.int32)[None, :]
    band_ids = jnp.arange(BANDS, dtype=jnp.int32)[:, None]
    dp_target = ranks // GROUP
    item_index = band_ids * GROUP + ranks % GROUP
    owners = dp_target * COLB + mp_perm[dp_target, item_index]
    flat_index = (band_ids * COLB + col_perm).reshape(-1)
    return jnp.zeros((NB,), jnp.int32).at[flat_index].set(owners.reshape(-1).astype(jnp.int32))


def setup_inputs(seed: int = 0) -> dict:
    seeds = jax.random.split(jax.random.key(seed), 7)
    grad = draw_grad(jax.random.fold_in(seeds[6], 71), 0)
    block_owner = draw_block_owner(jax.random.fold_in(seeds[6], 71), 0)
    left_stat = draw_left_stat(jax.random.fold_in(seeds[6], 71), 0)
    right_stat = draw_right_stat(jax.random.fold_in(seeds[6], 71), 0)
    left_root = draw_left_root(jax.random.fold_in(seeds[6], 71), 0)
    right_root = draw_right_root(jax.random.fold_in(seeds[6], 71), 0)
    return dict(grad=grad, block_owner=block_owner, left_stat=left_stat, right_stat=right_stat, left_root=left_root, right_root=right_root)


clip_level = 0.5
beta_stat = 0.95

def owner_step(items, scale):
    block, left_old, right_old, left_inv, right_inv = items
    left_gram = jnp.dot(block, block.T, preferred_element_type=jnp.float32)
    right_gram = jnp.dot(block.T, block, preferred_element_type=jnp.float32)
    factor = (1.0 - beta_stat) * scale * scale / BLK
    left_new = beta_stat * left_old + factor * left_gram
    right_new = beta_stat * right_old + factor * right_gram
    partial_left = jnp.dot(left_inv, block, preferred_element_type=jnp.float32).astype(jnp.bfloat16)
    update_block = (jnp.dot(partial_left, right_inv, preferred_element_type=jnp.float32) * scale).astype(jnp.bfloat16)
    return (left_new, right_new, update_block)

def reference(grad, block_owner, left_stat, right_stat, left_root, right_root):
    values = grad.astype(jnp.float32)
    mean_square = jnp.sum(values * values) / (ROWS * COLS)
    scale = clip_level / jnp.sqrt(mean_square + 1e-06)
    blocks = grad.reshape(BANDS, BLK, COLB, BLK).transpose(0, 2, 1, 3).reshape(NB, BLK, BLK)
    block_of = jnp.argsort(block_owner).astype(jnp.int32)
    owned = jnp.take(blocks, block_of, axis=0)
    new_left, new_right, updates = lax.map(lambda items: owner_step(items, scale), (owned, left_stat, right_stat, left_root, right_root))
    back = jnp.take(updates, block_owner.astype(jnp.int32), axis=0)
    update = back.reshape(BANDS, COLB, BLK, BLK).transpose(0, 2, 1, 3).reshape(ROWS, COLS)
    return (new_left, new_right, update)
```

```python
import functools

import jax
import jax.numpy as jnp
from jax import lax
from jax.experimental import pallas as pl
from jax.experimental.pallas import tpu as pltpu
from jax.sharding import PartitionSpec as P


clip_level = 0.5
beta_stat = 0.95

FORWARD = (2, 4, 2)
BACKWARD = (4, 2, 2)
ANY = pl.BlockSpec(memory_space=pl.ANY)


def spans(parts, size):
    total, at, out = sum(parts), 0, []
    for part in parts:
        out.append((at * size // total, part * size // total))
        at += part
    return out


def band_columns(owner, band, target, mp, group):
    count = jnp.int32(0)
    columns = [jnp.int32(0)] * group
    for c in range(mp):
        match = owner[band * mp + c] // mp == target
        for j in range(group):
            columns[j] = jnp.where(match & (count == j), c, columns[j])
        count = count + match.astype(jnp.int32)
    return columns


def call(body, outs, scratch, inputs, owner, name, aliases=None, flops=0, moved=1 << 22):
    return pl.pallas_call(
        body,
        out_shape=outs,
        in_specs=[pl.BlockSpec(memory_space=pltpu.SMEM)] + [ANY] * len(inputs),
        out_specs=[ANY] * len(outs),
        scratch_shapes=scratch,
        input_output_aliases=aliases or {},
        cost_estimate=pl.CostEstimate(flops=flops, bytes_accessed=moved, transcendentals=0),
        name=name,
    )(owner, *inputs)


def pack(grad, owner, dp, mp, blk, cuts):
    rows = grad.shape[0]
    group = mp // dp
    slots = (dp - 1) * group

    def body(owner, grad, *rest):
        outs, (buf, load, store) = rest[:-3], rest[-3:]
        me = lax.axis_index("dp")
        for k in range(1, dp):
            columns = band_columns(owner, me, me ^ k, mp, group)
            for j in range(group):
                slot = (k - 1) * group + j
                at = pl.multiple_of(columns[j] * blk, 128)
                pltpu.make_async_copy(grad.at[:, pl.ds(at, blk)], buf.at[slot], load.at[slot]).start()
        copies = []
        for k in range(1, dp):
            for j in range(group):
                slot = (k - 1) * group + j
                pltpu.make_async_copy(grad.at[:, pl.ds(0, blk)], buf.at[slot], load.at[slot]).wait()
                for c, (at, width) in enumerate(cuts):
                    copy = pltpu.make_async_copy(
                        buf.at[slot, :, pl.ds(at, width)],
                        outs[c * (dp - 1) + k - 1].at[j],
                        store.at[c * slots + slot],
                    )
                    copy.start()
                    copies.append(copy)
        for copy in copies:
            copy.wait()

    outs = [
        jax.ShapeDtypeStruct((group, rows, width), grad.dtype)
        for _, width in cuts
        for _ in range(dp - 1)
    ]
    scratch = [
        pltpu.VMEM((slots, rows, blk), grad.dtype),
        pltpu.SemaphoreType.DMA((slots,)),
        pltpu.SemaphoreType.DMA((slots * len(cuts),)),
    ]
    flat = call(body, outs, scratch, [grad], owner, "pack")
    return [flat[c * (dp - 1) : (c + 1) * (dp - 1)] for c in range(len(cuts))]


def fill_table(owner, table, me, dp, mp, group, local):
    for band in range(dp):
        count = jnp.int32(0)
        for c in range(mp):
            o = owner[band * mp + c]
            match = o // mp == me
            entry = (band ^ me) * group + count
            if local:
                entry = jnp.where(band == me, dp * group + c, entry)
            table[jnp.where(match, o % mp, mp)] = entry
            count = count + match.astype(jnp.int32)


def route(grad, got, owner, dp, mp, blk, at, width, name):
    rows = grad.shape[0]
    group = mp // dp

    def body(owner, grad, *rest):
        got, outs, (table, buf, load, store) = rest[: dp - 1], rest[dp - 1 : dp - 1 + mp], rest[dp - 1 + mp :]
        me, mine = lax.axis_index("dp"), lax.axis_index("mp")
        fill_table(owner, table, me, dp, mp, group, True)
        order = list(range(mp - 1, -1, -1))
        for kk in order:
            entry = table[mine ^ kk]
            for k in range(1, dp):

                @pl.when(entry // group == k)
                def _(k=k, kk=kk, entry=entry):
                    pltpu.make_async_copy(got[k - 1].at[entry % group], buf.at[kk], load.at[kk]).start()

            @pl.when(entry >= dp * group)
            def _(kk=kk, entry=entry):
                start = pl.multiple_of((entry - dp * group) * blk + at, 128)
                pltpu.make_async_copy(grad.at[:, pl.ds(start, width)], buf.at[kk], load.at[kk]).start()

        copies = []
        for kk in order:
            pltpu.make_async_copy(grad.at[:, pl.ds(0, width)], buf.at[kk], load.at[kk]).wait()
            copy = pltpu.make_async_copy(buf.at[kk], outs[kk], store.at[kk])
            copy.start()
            copies.append(copy)
        for copy in copies:
            copy.wait()

    outs = [jax.ShapeDtypeStruct((rows, width), grad.dtype)] * mp
    scratch = [
        pltpu.SMEM((mp + 1,), jnp.int32),
        pltpu.VMEM((mp, rows, width), grad.dtype),
        pltpu.SemaphoreType.DMA((mp,)),
        pltpu.SemaphoreType.DMA((mp,)),
    ]
    return call(body, outs, scratch, [grad, *got], owner, name)


def tile_rows(blk):
    return min(256, blk)


def partial_update(pieces, left_root, right_root, before, owner, mp, at, width, name):
    rows = pieces[0].shape[0]
    blk = left_root.shape[0]
    tile = tile_rows(blk)
    first = before is None

    def body(owner, *rest):
        rest = list(rest)
        parts = [rest.pop(0) for _ in range(mp)]
        left_ref, right_ref = rest.pop(0), rest.pop(0)
        old_ref = None if first else rest.pop(0)
        block_ref, new_ref = rest.pop(0), rest.pop(0)
        left, right, block, total, piece_sem, sems, out_sem = rest
        mine = lax.axis_index("mp")
        weights = [
            pltpu.make_async_copy(left_ref, left, sems.at[0]),
            pltpu.make_async_copy(right_ref.at[pl.ds(at, width), :], right, sems.at[1]),
        ]
        if not first:
            weights.append(pltpu.make_async_copy(old_ref, total, sems.at[2]))
        for copy in weights:
            copy.start()
        places = []
        for kk in range(mp):
            start = pl.multiple_of((mine ^ kk) * rows, 16)
            places.append(pltpu.make_async_copy(parts[kk], block.at[pl.ds(start, rows), :], piece_sem.at[kk]))
        for copy in places:
            copy.start()
        for copy in places:
            copy.wait()
        for copy in weights:
            copy.wait()
        out = pltpu.make_async_copy(block, block_ref, sems.at[3])
        out.start()

        @pl.loop(0, blk // tile)
        def _(i):
            span = pl.ds(pl.multiple_of(i * tile, tile), tile)
            half = jnp.dot(left[span, :], block[...], preferred_element_type=jnp.float32)
            term = jnp.dot(half.astype(block.dtype), right[...], preferred_element_type=jnp.float32)
            if first:
                total[span, :] = term
            else:
                total[span, :] = total[span, :] + term
            pltpu.make_async_copy(total.at[span, :], new_ref.at[span, :], out_sem.at[i]).start()

        for i in range(blk // tile):
            span = pl.ds(i * tile, tile)
            pltpu.make_async_copy(total.at[span, :], new_ref.at[span, :], out_sem.at[i]).wait()
        out.wait()

    outs = [
        jax.ShapeDtypeStruct((blk, width), pieces[0].dtype),
        jax.ShapeDtypeStruct((blk, blk), jnp.float32),
    ]
    scratch = [
        pltpu.VMEM((blk, blk), left_root.dtype),
        pltpu.VMEM((width, blk), right_root.dtype),
        pltpu.VMEM((blk, width), pieces[0].dtype),
        pltpu.VMEM((blk, blk), jnp.float32),
        pltpu.SemaphoreType.DMA((mp,)),
        pltpu.SemaphoreType.DMA((4,)),
        pltpu.SemaphoreType.DMA((blk // tile,)),
    ]
    inputs = [*pieces, left_root, right_root] + ([] if first else [before])
    return call(body, outs, scratch, inputs, owner, name, flops=2 * blk * blk * width * 2)


def last_update(pieces, left_root, right_root, before, scale, owner, mp, at, width, cuts, name):
    rows = pieces[0].shape[0]
    blk = left_root.shape[0]
    tile = tile_rows(blk)

    def body(owner, *rest):
        rest = list(rest)
        parts = [rest.pop(0) for _ in range(mp)]
        left_ref, right_ref, old_ref, scale_ref, block_ref = (rest.pop(0) for _ in range(5))
        outs = [rest.pop(0) for _ in range(mp * len(cuts))]
        left, right, block, total, update, factor, piece_sem, sems, out_sem = rest
        mine = lax.axis_index("mp")
        weights = [
            pltpu.make_async_copy(left_ref, left, sems.at[0]),
            pltpu.make_async_copy(right_ref.at[pl.ds(at, width), :], right, sems.at[1]),
            pltpu.make_async_copy(old_ref, total, sems.at[2]),
            pltpu.make_async_copy(scale_ref, factor, sems.at[4]),
        ]
        places = []
        for kk in range(mp):
            start = pl.multiple_of((mine ^ kk) * rows, 16)
            places.append(pltpu.make_async_copy(parts[kk], block.at[pl.ds(start, rows), :], piece_sem.at[kk]))
        for copy in places + weights:
            copy.start()
        for copy in places + weights:
            copy.wait()
        out = pltpu.make_async_copy(block, block_ref, sems.at[3])
        out.start()
        scaling = factor[0:1, 0:1]

        @pl.loop(0, blk // tile)
        def _(i):
            span = pl.ds(pl.multiple_of(i * tile, tile), tile)
            half = jnp.dot(left[span, :], block[...], preferred_element_type=jnp.float32)
            term = jnp.dot(half.astype(block.dtype), right[...], preferred_element_type=jnp.float32)
            update[span, :] = ((total[span, :] + term) * scaling).astype(update.dtype)

        copies = []
        for c, (start, size) in enumerate(cuts):
            for kk in range(mp):
                row = pl.multiple_of((mine ^ kk) * rows, 16)
                copies.append(
                    pltpu.make_async_copy(
                        update.at[pl.ds(row, rows), pl.ds(start, size)],
                        outs[c * mp + kk],
                        out_sem.at[c * mp + kk],
                    )
                )
        for copy in copies:
            copy.start()
        for copy in copies:
            copy.wait()
        out.wait()

    outs = [jax.ShapeDtypeStruct((blk, width), pieces[0].dtype)] + [
        jax.ShapeDtypeStruct((rows, size), pieces[0].dtype) for _, size in cuts for _ in range(mp)
    ]
    scratch = [
        pltpu.VMEM((blk, blk), left_root.dtype),
        pltpu.VMEM((width, blk), right_root.dtype),
        pltpu.VMEM((blk, width), pieces[0].dtype),
        pltpu.VMEM((blk, blk), jnp.float32),
        pltpu.VMEM((blk, blk), pieces[0].dtype),
        pltpu.VMEM((8, 128), jnp.float32),
        pltpu.SemaphoreType.DMA((mp,)),
        pltpu.SemaphoreType.DMA((5,)),
        pltpu.SemaphoreType.DMA((mp * len(cuts),)),
    ]
    inputs = [*pieces, left_root, right_root, before, scale]
    flat = call(body, outs, scratch, inputs, owner, name, flops=2 * blk * blk * width * 2)
    return flat[0], [flat[1 + c * mp : 1 + (c + 1) * mp] for c in range(len(cuts))]


def unroute(pieces, owner, dp, mp, name):
    rows, width = pieces[0].shape
    group = mp // dp

    def body(owner, *rest):
        pieces, outs, (table, buf, load, store) = rest[:mp], rest[mp : mp + dp], rest[mp + dp :]
        me, mine = lax.axis_index("dp"), lax.axis_index("mp")
        for kk in range(mp):
            pltpu.make_async_copy(pieces[kk], buf.at[kk], load.at[kk]).start()
        fill_table(owner, table, me, dp, mp, group, False)
        for kk in range(mp):
            pltpu.make_async_copy(pieces[kk], buf.at[kk], load.at[kk]).wait()
            entry = table[mine ^ kk]
            for k in range(dp):

                @pl.when(entry // group == k)
                def _(k=k, kk=kk, entry=entry):
                    pltpu.make_async_copy(buf.at[kk], outs[k].at[entry % group], store.at[kk]).start()

        for kk in range(mp):
            pltpu.make_async_copy(buf.at[kk], outs[0].at[0], store.at[kk]).wait()

    outs = [jax.ShapeDtypeStruct((group, rows, width), pieces[0].dtype)] * dp
    scratch = [
        pltpu.SMEM((mp + 1,), jnp.int32),
        pltpu.VMEM((mp, rows, width), pieces[0].dtype),
        pltpu.SemaphoreType.DMA((mp,)),
        pltpu.SemaphoreType.DMA((mp,)),
    ]
    return call(body, outs, scratch, list(pieces), owner, name)


def place(parts, before, owner, dp, mp, blk, at, name):
    group, rows, width = parts[0].shape
    slots = dp * group

    def body(owner, *rest):
        parts = rest[:dp]
        out, buf, load, store = rest[-4:]
        me = lax.axis_index("dp")
        for k in range(dp):
            for j in range(group):
                slot = k * group + j
                pltpu.make_async_copy(parts[k].at[j], buf.at[slot], load.at[slot]).start()
        copies = []
        for k in range(dp):
            columns = band_columns(owner, me, me ^ k, mp, group)
            for j in range(group):
                slot = k * group + j
                pltpu.make_async_copy(parts[k].at[j], buf.at[slot], load.at[slot]).wait()
                start = pl.multiple_of(columns[j] * blk + at, 128)
                copy = pltpu.make_async_copy(buf.at[slot], out.at[:, pl.ds(start, width)], store.at[slot])
                copy.start()
                copies.append(copy)
        for copy in copies:
            copy.wait()

    outs = [jax.ShapeDtypeStruct((rows, mp * blk), parts[0].dtype)]
    scratch = [
        pltpu.VMEM((slots, rows, width), parts[0].dtype),
        pltpu.SemaphoreType.DMA((slots,)),
        pltpu.SemaphoreType.DMA((slots,)),
    ]
    inputs = list(parts) + ([] if before is None else [before])
    aliases = {} if before is None else {1 + dp: 0}
    return call(body, outs, scratch, inputs, owner, name, aliases)[0]


def swap(value, axis, distance):
    count = lax.axis_size(axis)
    return lax.ppermute(value, axis, [(i, i ^ distance) for i in range(count)])


def all_sum(value, dp, mp):
    total = jnp.broadcast_to(value, (8, 128))
    for axis, count in (("mp", mp), ("dp", dp)):
        step = 1
        while step < count:
            total = total + swap(total, axis, step)
            step *= 2
    return total


def far_first(count):
    return list(range(count // 2, count)) + list(range(1, count // 2))


def per_device(grad, owner, left_stat, right_stat, left_root, right_root):
    dp, mp = lax.axis_size("dp"), lax.axis_size("mp")
    blk = left_root.shape[-1]
    left_root, right_root = left_root[0], right_root[0]
    forward, backward = spans(FORWARD, blk), spans(BACKWARD, blk)

    packed = pack(grad, owner, dp, mp, blk, forward)
    crossed = [[swap(part, "dp", k + 1) for k, part in enumerate(chunk)] for chunk in packed]
    values = grad.astype(jnp.float32)
    total = all_sum(jnp.sum(values * values), dp, mp)
    mean_square = total / (grad.size * dp * mp)
    scale = clip_level / jnp.sqrt(mean_square + 1e-06)

    arrived = []
    for c, (at, width) in enumerate(forward):
        pieces = route(grad, crossed[c], owner, dp, mp, blk, at, width, f"route{c}")
        moved = list(pieces)
        for k in far_first(mp):
            moved[k] = swap(pieces[k], "mp", k)
        arrived.append(moved)

    blocks, update = [], None
    for c, (at, width) in enumerate(forward[:-1]):
        block, update = partial_update(
            arrived[c], left_root, right_root, update, owner, mp, at, width, f"partial{c}"
        )
        blocks.append(block)
    at, width = forward[-1]
    block, leaving = last_update(
        arrived[-1], left_root, right_root, update, scale, owner, mp, at, width, backward, "last"
    )
    blocks.append(block)

    out = None
    for c, (at, width) in enumerate(backward):
        pieces = list(leaving[c])
        for k in far_first(mp):
            pieces[k] = swap(leaving[c][k], "mp", k)
        parts = list(unroute(pieces, owner, dp, mp, f"unroute{c}"))
        for k in range(1, dp):
            parts[k] = swap(parts[k], "dp", k)
        out = place(parts, out, owner, dp, mp, blk, at, f"place{c}")

    block = jnp.concatenate(blocks, axis=1)
    factor = ((1.0 - beta_stat) * scale * scale / blk)[0, 0]
    left_gram = jnp.dot(block, block.T, preferred_element_type=jnp.float32)
    right_gram = jnp.dot(block.T, block, preferred_element_type=jnp.float32)
    left_new = beta_stat * left_stat[0] + factor * left_gram
    right_new = beta_stat * right_stat[0] + factor * right_gram
    return (left_new[None], right_new[None], out)


def solution(mesh):
    split = P(("dp", "mp"), None, None)
    rows = P(("dp", "mp"), None)
    return jax.shard_map(
        per_device,
        mesh=mesh,
        in_specs=(rows, P(), split, split, split, split),
        out_specs=(split, split, rows),
        check_vma=False,
    )
```

```python
import jax
import jax.numpy as jnp
from jax import lax
from jax.experimental import pallas as pl
from jax.experimental.pallas import tpu as pltpu
from jax.sharding import PartitionSpec as P


clip_level = 0.5
beta_stat = 0.95

FORWARD = (3, 5)
BACKWARD = (3, 3, 2)
ANY = pl.BlockSpec(memory_space=pl.ANY)
SMEM = pl.BlockSpec(memory_space=pltpu.SMEM)
VMEM = pl.BlockSpec(memory_space=pltpu.VMEM)
HBM = pl.BlockSpec(memory_space=pltpu.HBM)


def spans(parts, size):
    total, at, out = sum(parts), 0, []
    for part in parts:
        out.append((at * size // total, part * size // total))
        at += part
    return out


def band_columns(owner, band, target, mp, group):
    count = jnp.int32(0)
    columns = [jnp.int32(0)] * group
    for c in range(mp):
        match = owner[band * mp + c] // mp == target
        for j in range(group):
            columns[j] = jnp.where(match & (count == j), c, columns[j])
        count = count + match.astype(jnp.int32)
    return columns


def call(body, outs, inputs, owner, scratch=(), ins=VMEM, out=VMEM, aliases=None, flops=0, mib=8):
    ins = ins if isinstance(ins, list) else [ins] * len(inputs)
    return pl.pallas_call(
        body,
        out_shape=outs,
        in_specs=[SMEM] + ins,
        out_specs=[out] * len(outs),
        scratch_shapes=list(scratch),
        input_output_aliases=aliases or {},
        cost_estimate=pl.CostEstimate(flops=flops, bytes_accessed=1 << 21, transcendentals=0),
        compiler_params=pltpu.CompilerParams(vmem_limit_bytes=mib << 20),
    )(owner, *inputs)


def pack(grad, owner, dp, mp, blk, cuts):
    rows = grad.shape[0]
    group = mp // dp

    def body(owner, grad, *rest):
        outs, sems = rest[:-1], rest[-1]
        me = lax.axis_index("dp")
        copies = []
        for k in list(range(1, dp)) + [0]:
            columns = band_columns(owner, me, me ^ k, mp, group)
            for j in range(group):
                for c, (at, width) in enumerate(cuts):
                    start = pl.multiple_of(columns[j] * blk + at, 128)
                    copy = pltpu.make_async_copy(
                        grad.at[:, pl.ds(start, width)],
                        outs[c * dp + k].at[j],
                        sems.at[(c * dp + k) * group + j],
                    )
                    copy.start()
                    copies.append(copy)
        for copy in copies:
            copy.wait()

    outs = [jax.ShapeDtypeStruct((group, rows, width), grad.dtype) for _, width in cuts for _ in range(dp)]
    scratch = [pltpu.SemaphoreType.DMA((mp * len(cuts),))]
    grad = pltpu.with_memory_space_constraint(grad, pltpu.HBM)
    flat = call(body, outs, [grad], owner, scratch, ins=HBM)
    return [flat[c * dp : (c + 1) * dp] for c in range(len(cuts))]


def square_sum(grad, owner):
    rows, cols = grad.shape
    step = min(1024, cols)

    def body(owner, grad, out):
        total = jnp.zeros((8, step), jnp.float32)
        for i in range(cols // step):
            values = grad[:, i * step : (i + 1) * step].astype(jnp.float32)
            total = total + jnp.sum((values * values).reshape(rows // 8, 8, step), axis=0)
        out[...] = jnp.full(out.shape, jnp.sum(total), jnp.float32)

    return call(body, [jax.ShapeDtypeStruct((8, 128), jnp.float32)], [grad], owner)[0]


def fill_table(owner, table, me, dp, mp, group):
    for band in range(dp):
        count = jnp.int32(0)
        for c in range(mp):
            o = owner[band * mp + c]
            match = o // mp == me
            table[jnp.where(match, o % mp, mp)] = (band ^ me) * group + count
            count = count + match.astype(jnp.int32)


def route(got, owner, dp, mp):
    group, rows, width = got[0].shape

    def body(owner, *rest):
        got, outs, table = rest[:dp], rest[dp : dp + mp], rest[dp + mp]
        fill_table(owner, table, lax.axis_index("dp"), dp, mp, group)
        mine = lax.axis_index("mp")
        for kk in range(mp):
            entry = table[mine ^ kk]
            for k in range(dp):

                @pl.when(entry // group == k)
                def _(k=k, kk=kk, entry=entry):
                    outs[kk][...] = got[k][entry % group]

    outs = [jax.ShapeDtypeStruct((rows, width), got[0].dtype)] * mp
    return call(body, outs, got, owner, [pltpu.SMEM((mp + 1,), jnp.int32)])


def unroute(pieces, owner, dp, mp):
    rows, width = pieces[0].shape
    group = mp // dp

    def body(owner, *rest):
        pieces, outs, table = rest[:mp], rest[mp : mp + dp], rest[mp + dp]
        fill_table(owner, table, lax.axis_index("dp"), dp, mp, group)
        mine = lax.axis_index("mp")
        for kk in range(mp):
            entry = table[mine ^ kk]
            for k in range(dp):

                @pl.when(entry // group == k)
                def _(k=k, kk=kk, entry=entry):
                    outs[k][entry % group] = pieces[kk][...]

    outs = [jax.ShapeDtypeStruct((group, rows, width), pieces[0].dtype)] * dp
    return call(body, outs, list(pieces), owner, [pltpu.SMEM((mp + 1,), jnp.int32)])


def place(parts, owner, dp, mp, blk, cuts):
    group, rows = parts[0][0].shape[:2]
    count = len(cuts)

    def body(owner, *rest):
        parts, out, sems = rest[: count * dp], rest[-2], rest[-1]
        me = lax.axis_index("dp")
        copies = []
        for k in range(dp):
            columns = band_columns(owner, me, me ^ k, mp, group)
            for j in range(group):
                for c, (at, width) in enumerate(cuts):
                    start = pl.multiple_of(columns[j] * blk + at, 128)
                    copy = pltpu.make_async_copy(
                        parts[c * dp + k].at[j],
                        out.at[:, pl.ds(start, width)],
                        sems.at[(c * dp + k) * group + j],
                    )
                    copy.start()
                    copies.append(copy)
        for copy in copies:
            copy.wait()

    outs = [jax.ShapeDtypeStruct((rows, mp * blk), parts[0][0].dtype)]
    inputs = [part for chunk in parts for part in chunk]
    scratch = [pltpu.SemaphoreType.DMA((mp * count,))]
    return call(body, outs, inputs, owner, scratch, VMEM, ANY)[0]


def gather(pieces, block, mp, at, width):
    rows = pieces[0].shape[0]
    mine = lax.axis_index("mp")
    for kk in range(mp):
        start = pl.multiple_of((mine ^ kk) * rows, 16)
        block[pl.ds(start, rows), at : at + width] = pieces[kk][...]


def partial_update(pieces, left_root, right_root, old, owner, mp, at, width):
    blk = left_root.shape[0]
    tile = min(512, blk)

    def body(owner, *rest):
        pieces = rest[:mp]
        left, right = rest[mp : mp + 2]
        block, total = rest[-2:]
        gather(pieces, block, mp, at, width)

        @pl.loop(0, blk // tile)
        def _(i):
            span = pl.ds(pl.multiple_of(i * tile, tile), tile)
            half = jnp.dot(left[span, :], block[:, at : at + width], preferred_element_type=jnp.float32)
            term = jnp.dot(
                half.astype(block.dtype), right[at : at + width, :], preferred_element_type=jnp.float32
            )
            total[span, :] = term if old is None else total[span, :] + term

    outs = [
        jax.ShapeDtypeStruct((blk, blk), pieces[0].dtype),
        jax.ShapeDtypeStruct((blk, blk), jnp.float32),
    ]
    inputs = [*pieces, left_root, right_root, *(old or ())]
    aliases = None if old is None else {mp + 3: 0, mp + 4: 1}
    return call(body, outs, inputs, owner, aliases=aliases, flops=4 * blk * blk * width, mib=24)


def deal(update, outs, rows, mp, cuts):
    mine = lax.axis_index("mp")
    for c, (start, size) in enumerate(cuts):
        for kk in range(mp):
            row = pl.multiple_of((mine ^ kk) * rows, 16)
            outs[c * mp + kk][...] = update[pl.ds(row, rows), start : start + size]


def last_update(pieces, left_root, right_root, block, total, scale, owner, mp, at, width, cut):
    rows = pieces[0].shape[0]
    blk = left_root.shape[0]
    tile = min(512, blk)
    start, size = cut

    def body(owner, *rest):
        pieces = rest[:mp]
        left, right, total, scale, _, block, half = rest[mp : mp + 7]
        outs, update = rest[mp + 7 : -1], rest[-1]
        gather(pieces, block, mp, at, width)
        scaling = scale[0:1, 0:1]

        @pl.loop(0, blk // tile)
        def _(i):
            span = pl.ds(pl.multiple_of(i * tile, tile), tile)
            term = jnp.dot(left[span, :], block[:, at : at + width], preferred_element_type=jnp.float32)
            half[span, :] = term.astype(half.dtype)
            term = jnp.dot(
                term.astype(half.dtype),
                right[at : at + width, start : start + size],
                preferred_element_type=jnp.float32,
            )
            update[span, :] = ((total[span, start : start + size] + term) * scaling).astype(update.dtype)

        deal(update, outs, rows, mp, [(0, size)])

    dtype = pieces[0].dtype
    outs = [jax.ShapeDtypeStruct((blk, blk), dtype), jax.ShapeDtypeStruct((blk, width), dtype)]
    outs += [jax.ShapeDtypeStruct((rows, size), dtype)] * mp
    scratch = [pltpu.VMEM((blk, size), dtype)]
    inputs = [*pieces, left_root, right_root, total, scale, block]
    flops = 2 * blk * width * (blk + size)
    flat = call(body, outs, inputs, owner, scratch, aliases={mp + 5: 0}, flops=flops, mib=24)
    return flat[0], flat[1], flat[2:]


def rest_update(half, right_root, total, scale, rows, owner, mp, at, cuts):
    blk, width = half.shape
    tile = min(512, blk)
    base = cuts[0][0]

    def body(owner, half, right, total, scale, *rest):
        outs, update = rest[:-1], rest[-1]
        scaling = scale[0:1, 0:1]

        @pl.loop(0, blk // tile)
        def _(i):
            span = pl.ds(pl.multiple_of(i * tile, tile), tile)
            term = jnp.dot(half[span, :], right[at : at + width, base:], preferred_element_type=jnp.float32)
            update[span, :] = ((total[span, base:] + term) * scaling).astype(update.dtype)

        deal(update, outs, rows, mp, [(start - base, size) for start, size in cuts])

    outs = [jax.ShapeDtypeStruct((rows, size), half.dtype) for _, size in cuts for _ in range(mp)]
    scratch = [pltpu.VMEM((blk, blk - base), half.dtype)]
    flops = 2 * blk * width * (blk - base)
    flat = call(body, outs, [half, right_root, total, scale], owner, scratch, flops=flops, mib=24)
    return [flat[c * mp : (c + 1) * mp] for c in range(len(cuts))]


def swap(value, axis, distance):
    count = lax.axis_size(axis)
    return lax.ppermute(value, axis, [(i, i ^ distance) for i in range(count)])


def far_first(count):
    return list(range(count // 2, count)) + list(range(1, count // 2))


def steps(count):
    step = 1
    while step < count:
        yield step
        step *= 2


def per_device(grad, owner, left_stat, right_stat, left_root, right_root):
    dp, mp = lax.axis_size("dp"), lax.axis_size("mp")
    blk = left_root.shape[-1]
    left_root, right_root = left_root[0], right_root[0]
    forward, backward = spans(FORWARD, blk), spans(BACKWARD, blk)

    packed = pack(grad, owner, dp, mp, blk, forward)
    crossed = [[part if k == 0 else swap(part, "dp", k) for k, part in enumerate(chunk)] for chunk in packed]
    total = square_sum(grad, owner)
    total = total + swap(total, "mp", 1)
    terms = [swap(total, "mp", k) for k in range(2, mp, 2)]
    total = sum(terms, total)
    for step in steps(dp):
        total = total + swap(total, "dp", step)
    mean_square = total / (grad.size * dp * mp)
    scale = clip_level / jnp.sqrt(mean_square + 1e-06)

    arrived = []
    for c in range(len(forward)):
        pieces = route(crossed[c], owner, dp, mp)
        moved = list(pieces)
        for k in far_first(mp):
            moved[k] = swap(pieces[k], "mp", k)
        arrived.append(moved)

    state = None
    for c, (at, width) in enumerate(forward[:-1]):
        state = partial_update(arrived[c], left_root, right_root, state, owner, mp, at, width)
    at, width = forward[-1]
    rows = arrived[0][0].shape[0]
    block, half, first = last_update(
        arrived[-1], left_root, right_root, *state, scale, owner, mp, at, width, backward[0]
    )
    leaving = [first] + rest_update(half, right_root, state[1], scale, rows, owner, mp, at, backward[1:])

    parts = []
    for c in range(len(backward)):
        pieces = list(leaving[c])
        for k in far_first(mp):
            pieces[k] = swap(leaving[c][k], "mp", k)
        chunk = list(unroute(pieces, owner, dp, mp))
        for k in range(1, dp):
            chunk[k] = swap(chunk[k], "dp", k)
        parts.append(chunk)
    out = place(parts, owner, dp, mp, blk, backward)

    factor = ((1.0 - beta_stat) * scale * scale / blk)[0, 0]
    left_gram = jnp.dot(block, block.T, preferred_element_type=jnp.float32)
    left_new = beta_stat * left_stat[0] + factor * left_gram
    right_gram = jnp.dot(block.T, block, preferred_element_type=jnp.float32)
    right_new = beta_stat * right_stat[0] + factor * right_gram
    return (left_new[None], right_new[None], out)


def solution(mesh):
    split = P(("dp", "mp"), None, None)
    rows = P(("dp", "mp"), None)

    return jax.shard_map(
        per_device,
        mesh=mesh,
        in_specs=(rows, P(), split, split, split, split),
        out_specs=(split, split, rows),
        check_vma=False,
    )
```

```python
import jax
import jax.numpy as jnp
from jax import lax
from jax.experimental import pallas as pl
from jax.experimental.pallas import tpu as pltpu
from jax.sharding import PartitionSpec as P


clip_level = 0.5
beta_stat = 0.95

FORWARD = (2, 4, 2)
BACKWARD = (4, 2, 2)
ANY = pl.BlockSpec(memory_space=pl.ANY)
SMEM = pl.BlockSpec(memory_space=pltpu.SMEM)
VMEM = pl.BlockSpec(memory_space=pltpu.VMEM)
HBM = pl.BlockSpec(memory_space=pltpu.HBM)


def spans(parts, size):
    total, at, out = sum(parts), 0, []
    for part in parts:
        out.append((at * size // total, part * size // total))
        at += part
    return out


def high(value, count):
    return value >> (count.bit_length() - 1) if count & (count - 1) == 0 else value // count


def low(value, count):
    return value & (count - 1) if count & (count - 1) == 0 else value % count


def column_slots(owner, me, mp, group):
    distances = [high(owner[me * mp + c], mp) ^ me for c in range(mp)]
    return [
        k * group + sum([(other == k).astype(jnp.int32) for other in distances[:c]], jnp.int32(0))
        for c, k in enumerate(distances)
    ]


def list_slots(owner, slots, me, dp, mp, group):
    owners = [owner[b] for b in range(dp * mp)]
    found = []
    for band in range(dp):
        last = [jnp.int32(0)] * group
        for o in owners[band * mp : (band + 1) * mp]:
            match = high(o, mp) == me
            last = [jnp.where(match, new, old) for new, old in zip(last[1:] + [low(o, mp)], last)]
        found.append(last)
    for band in range(dp):
        for rank, m in enumerate(found[band]):
            slots[m] = (band ^ me) * group + rank


def call(body, outs, inputs, table, scratch=(), ins=VMEM, out=VMEM, aliases=None, flops=0, mib=8):
    ins = ins if isinstance(ins, list) else [ins] * len(inputs)
    out = out if isinstance(out, list) else [out] * len(outs)
    return pl.pallas_call(
        body,
        out_shape=outs,
        in_specs=[SMEM] + ins,
        out_specs=out,
        scratch_shapes=list(scratch),
        input_output_aliases=aliases or {},
        cost_estimate=pl.CostEstimate(flops=flops, bytes_accessed=1 << 21, transcendentals=0),
        compiler_params=pltpu.CompilerParams(vmem_limit_bytes=mib << 20),
    )(table, *inputs)


def pack_first(grad, owner, dp, mp, blk, cut):
    rows = grad.shape[0]
    group = mp // dp
    at, width = cut

    def body(grad, owner_ref, *rest):
        outs, (plan, owner, buf, sems) = rest[:dp], rest[dp:]
        table = pltpu.make_async_copy(owner_ref, owner, sems.at[mp])
        table.start()
        copies = [
            pltpu.make_async_copy(grad.at[:, pl.ds(c * blk + at, width)], buf.at[c], sems.at[c])
            for c in range(mp)
        ]
        for copy in copies:
            copy.start()
        table.wait()
        slots = column_slots(owner, lax.axis_index("dp"), mp, group)
        for c, slot in enumerate(slots):
            plan[slot] = c
        for c, slot in enumerate(slots):
            copies[c].wait()
            for k in range(dp):

                @pl.when(high(slot, group) == k)
                def _(k=k, c=c, slot=slot):
                    outs[k][low(slot, group)] = buf[c]

    outs = [jax.ShapeDtypeStruct((group, rows, width), grad.dtype)] * dp
    outs.append(jax.ShapeDtypeStruct((mp,), jnp.int32))
    flat = pl.pallas_call(
        body,
        out_shape=outs,
        in_specs=[HBM, HBM],
        out_specs=[VMEM] * dp + [SMEM],
        scratch_shapes=[
            pltpu.SMEM(owner.shape, jnp.int32),
            pltpu.VMEM((mp, rows, width), grad.dtype),
            pltpu.SemaphoreType.DMA((mp + 1,)),
        ],
        cost_estimate=pl.CostEstimate(flops=0, bytes_accessed=1 << 21, transcendentals=0),
        compiler_params=pltpu.CompilerParams(vmem_limit_bytes=8 << 20),
        name="pack0",
    )(
        pltpu.with_memory_space_constraint(grad, pltpu.HBM),
        pltpu.with_memory_space_constraint(owner, pltpu.HBM),
    )
    return flat[:dp], flat[dp]


def pack(grad, plan, owner, dp, mp, blk, cut):
    rows = grad.shape[0]
    group = mp // dp
    at, width = cut

    def body(plan, grad, *rest):
        rest = list(rest)
        owner_ref = None if owner is None else rest.pop(0)
        outs, sems = rest[:dp], rest[-1]
        copies = []
        for k in list(range(1, dp)) + [0]:
            for j in range(group):
                start = pl.multiple_of(plan[k * group + j] * blk + at, 128)
                copy = pltpu.make_async_copy(
                    grad.at[:, pl.ds(start, width)], outs[k].at[j], sems.at[k * group + j]
                )
                copy.start()
                copies.append(copy)
        if owner is not None:
            list_slots(owner_ref, rest[dp], lax.axis_index("dp"), dp, mp, group)
        for copy in copies:
            copy.wait()

    outs = [jax.ShapeDtypeStruct((group, rows, width), grad.dtype)] * dp
    out, inputs, ins = [VMEM] * dp, [pltpu.with_memory_space_constraint(grad, pltpu.HBM)], [HBM]
    if owner is not None:
        outs.append(jax.ShapeDtypeStruct((mp,), jnp.int32))
        out, inputs, ins = out + [SMEM], inputs + [owner], ins + [SMEM]
    flat = call(body, outs, inputs, plan, [pltpu.SemaphoreType.DMA((mp,))], ins=ins, out=out)
    return flat[:dp], flat[dp:]


def square_sum(grad, plan):
    rows, cols = grad.shape
    step = min(1024, cols)

    def body(plan, grad, out):
        total = jnp.zeros((8, step), jnp.float32)
        for i in range(cols // step):
            values = grad[:, i * step : (i + 1) * step].astype(jnp.float32)
            total = total + jnp.sum((values * values).reshape(rows // 8, 8, step), axis=0)
        out[...] = jnp.full(out.shape, jnp.sum(total), jnp.float32)

    return call(body, [jax.ShapeDtypeStruct((8, 128), jnp.float32)], [grad], plan)[0]


def route(got, plan, dp, mp):
    group, rows, width = got[0].shape

    def body(plan, *rest):
        got, outs = rest[:dp], rest[dp:]
        mine = lax.axis_index("mp")
        for kk in range(mp):
            entry = plan[mine ^ kk]
            for k in range(dp):

                @pl.when(high(entry, group) == k)
                def _(k=k, kk=kk, entry=entry):
                    outs[kk][...] = got[k][low(entry, group)]

    outs = [jax.ShapeDtypeStruct((rows, width), got[0].dtype)] * mp
    return call(body, outs, got, plan)


def unroute(pieces, plan, dp, mp):
    rows, width = pieces[0].shape
    group = mp // dp

    def body(plan, *rest):
        pieces, outs = rest[:mp], rest[mp:]
        mine = lax.axis_index("mp")
        for kk in range(mp):
            entry = plan[mine ^ kk]
            for k in range(dp):

                @pl.when(high(entry, group) == k)
                def _(k=k, kk=kk, entry=entry):
                    outs[k][low(entry, group)] = pieces[kk][...]

    outs = [jax.ShapeDtypeStruct((group, rows, width), pieces[0].dtype)] * dp
    return call(body, outs, list(pieces), plan)


def place(parts, old, plan, dp, mp, blk, cuts):
    group, rows = parts[0][0].shape[:2]
    count = len(cuts)

    def body(plan, *rest):
        parts, out, sems = rest[: count * dp], rest[-2], rest[-1]
        copies = []
        for k in range(dp):
            for j in range(group):
                for c, (at, width) in enumerate(cuts):
                    start = pl.multiple_of(plan[k * group + j] * blk + at, 128)
                    copy = pltpu.make_async_copy(
                        parts[c * dp + k].at[j],
                        out.at[:, pl.ds(start, width)],
                        sems.at[(c * dp + k) * group + j],
                    )
                    copy.start()
                    copies.append(copy)
        for copy in copies:
            copy.wait()

    outs = [jax.ShapeDtypeStruct((rows, mp * blk), parts[0][0].dtype)]
    inputs = [part for chunk in parts for part in chunk]
    ins = [VMEM] * len(inputs)
    aliases = None
    if old is not None:
        aliases = {1 + len(inputs): 0}
        inputs, ins = inputs + [old], ins + [ANY]
    scratch = [pltpu.SemaphoreType.DMA((mp * count,))]
    return call(body, outs, inputs, plan, scratch, ins, ANY, aliases)[0]


def gather(pieces, block, mp, at, width):
    rows = pieces[0].shape[0]
    mine = lax.axis_index("mp")
    for kk in range(mp):
        start = pl.multiple_of((mine ^ kk) * rows, 16)
        block[pl.ds(start, rows), at : at + width] = pieces[kk][...]


def partial_update(pieces, left_root, right_root, old, plan, mp, at, width):
    blk = left_root.shape[0]
    tile = min(512, blk)

    def body(plan, *rest):
        pieces = rest[:mp]
        left, right = rest[mp : mp + 2]
        block, total = rest[-2:]
        gather(pieces, block, mp, at, width)

        @pl.loop(0, blk // tile)
        def _(i):
            span = pl.ds(pl.multiple_of(i * tile, tile), tile)
            half = jnp.dot(left[span, :], block[:, at : at + width], preferred_element_type=jnp.float32)
            term = jnp.dot(
                half.astype(block.dtype), right[at : at + width, :], preferred_element_type=jnp.float32
            )
            total[span, :] = term if old is None else total[span, :] + term

    outs = [
        jax.ShapeDtypeStruct((blk, blk), pieces[0].dtype),
        jax.ShapeDtypeStruct((blk, blk), jnp.float32),
    ]
    inputs = [*pieces, left_root, right_root, *(old or ())]
    aliases = None if old is None else {mp + 3: 0, mp + 4: 1}
    return call(body, outs, inputs, plan, aliases=aliases, flops=4 * blk * blk * width, mib=24)


def deal(update, outs, rows, mp, cuts):
    mine = lax.axis_index("mp")
    for c, (start, size) in enumerate(cuts):
        for kk in range(mp):
            row = pl.multiple_of((mine ^ kk) * rows, 16)
            outs[c * mp + kk][...] = update[pl.ds(row, rows), start : start + size]


def last_update(pieces, left_root, right_root, block, total, scale, plan, mp, at, width, cut):
    rows = pieces[0].shape[0]
    blk = left_root.shape[0]
    tile = min(512, blk)
    start, size = cut

    def body(plan, *rest):
        pieces = rest[:mp]
        left, right, total, scale, _, block, half = rest[mp : mp + 7]
        outs, update = rest[mp + 7 : -1], rest[-1]
        gather(pieces, block, mp, at, width)
        scaling = scale[0:1, 0:1]

        @pl.loop(0, blk // tile)
        def _(i):
            span = pl.ds(pl.multiple_of(i * tile, tile), tile)
            term = jnp.dot(left[span, :], block[:, at : at + width], preferred_element_type=jnp.float32)
            half[span, :] = term.astype(half.dtype)
            term = jnp.dot(
                term.astype(half.dtype),
                right[at : at + width, start : start + size],
                preferred_element_type=jnp.float32,
            )
            update[span, :] = ((total[span, start : start + size] + term) * scaling).astype(update.dtype)

        deal(update, outs, rows, mp, [(0, size)])

    dtype = pieces[0].dtype
    outs = [jax.ShapeDtypeStruct((blk, blk), dtype), jax.ShapeDtypeStruct((blk, width), dtype)]
    outs += [jax.ShapeDtypeStruct((rows, size), dtype)] * mp
    scratch = [pltpu.VMEM((blk, size), dtype)]
    inputs = [*pieces, left_root, right_root, total, scale, block]
    flops = 2 * blk * width * (blk + size)
    flat = call(body, outs, inputs, plan, scratch, aliases={mp + 5: 0}, flops=flops, mib=24)
    return flat[0], flat[1], flat[2:]


def rest_update(half, right_root, total, scale, rows, plan, mp, at, cuts):
    blk, width = half.shape
    tile = min(512, blk)
    base = cuts[0][0]

    def body(plan, half, right, total, scale, *rest):
        outs, update = rest[:-1], rest[-1]
        scaling = scale[0:1, 0:1]

        @pl.loop(0, blk // tile)
        def _(i):
            span = pl.ds(pl.multiple_of(i * tile, tile), tile)
            term = jnp.dot(half[span, :], right[at : at + width, base:], preferred_element_type=jnp.float32)
            update[span, :] = ((total[span, base:] + term) * scaling).astype(update.dtype)

        deal(update, outs, rows, mp, [(start - base, size) for start, size in cuts])

    outs = [jax.ShapeDtypeStruct((rows, size), half.dtype) for _, size in cuts for _ in range(mp)]
    scratch = [pltpu.VMEM((blk, blk - base), half.dtype)]
    flops = 2 * blk * width * (blk - base)
    flat = call(body, outs, [half, right_root, total, scale], plan, scratch, flops=flops, mib=24)
    return [flat[c * mp : (c + 1) * mp] for c in range(len(cuts))]


def swap(value, axis, distance):
    count = lax.axis_size(axis)
    return lax.ppermute(value, axis, [(i, i ^ distance) for i in range(count)])


def per_device(grad, owner, left_stat, right_stat, left_root, right_root):
    dp, mp = lax.axis_size("dp"), lax.axis_size("mp")
    blk = left_root.shape[-1]
    left_root, right_root = left_root[0], right_root[0]
    forward, backward = spans(FORWARD, blk), spans(BACKWARD, blk)

    chunk, plan = pack_first(grad, owner, dp, mp, blk, forward[0])
    packed, slots = [chunk], None
    for c, cut in enumerate(forward[1:], 1):
        chunk, found = pack(grad, plan, owner if slots is None else None, dp, mp, blk, cut)
        packed.append(chunk)
        slots = found[0] if found else slots
    crossed = [[part if k == 0 else swap(part, "dp", k) for k, part in enumerate(chunk)] for chunk in packed]
    total = square_sum(grad, plan)
    total = total + swap(total, "mp", 1)
    terms = [swap(total, "mp", k) for k in range(2, mp, 2)]
    total = sum(terms, total)
    terms = [swap(total, "dp", k) for k in range(1, dp)]
    total = sum(terms, total)
    mean_square = total / (grad.size * dp * mp)
    scale = clip_level / jnp.sqrt(mean_square + 1e-06)
    factor = (1.0 - beta_stat) * scale * scale / blk

    arrived = []
    for c in range(len(forward)):
        pieces = route(crossed[c], slots, dp, mp)
        moved = list(pieces)
        for k in range(1, mp):
            moved[k] = swap(pieces[k], "mp", k)
        arrived.append(moved)

    state = None
    for c, (at, width) in enumerate(forward[:-1]):
        state = partial_update(arrived[c], left_root, right_root, state, plan, mp, at, width)
    at, width = forward[-1]
    rows = arrived[0][0].shape[0]
    block, half, first = last_update(
        arrived[-1], left_root, right_root, *state, scale, plan, mp, at, width, backward[0]
    )
    leaving = [first] + rest_update(half, right_root, state[1], scale, rows, plan, mp, at, backward[1:])

    parts = []
    for c in range(len(backward)):
        pieces = list(leaving[c])
        for k in range(1, mp):
            pieces[k] = swap(leaving[c][k], "mp", k)
        chunk = list(unroute(pieces, slots, dp, mp))
        for k in range(1, dp):
            chunk[k] = swap(chunk[k], "dp", k)
        parts.append(chunk)
    out = place(parts[:-1], None, plan, dp, mp, blk, backward[:-1])
    out = place(parts[-1:], out, plan, dp, mp, blk, backward[-1:])

    factor = factor[0, 0]
    left_gram = jnp.dot(block, block.T, preferred_element_type=jnp.float32)
    left_new = beta_stat * left_stat[0] + factor * left_gram
    right_gram = jnp.dot(block.T, block, preferred_element_type=jnp.float32)
    right_new = beta_stat * right_stat[0] + factor * right_gram
    return (left_new[None], right_new[None], out)


def solution(mesh):
    split = P(("dp", "mp"), None, None)
    rows = P(("dp", "mp"), None)

    return jax.shard_map(
        per_device,
        mesh=mesh,
        in_specs=(rows, P(), split, split, split, split),
        out_specs=(split, split, rows),
        check_vma=False,
    )
```

```python
import jax
import jax.numpy as jnp
from jax import lax
from jax.experimental import pallas as pl
from jax.experimental.pallas import tpu as pltpu
from jax.sharding import PartitionSpec as P


clip_level = 0.5
beta_stat = 0.95

FORWARD = (2, 4, 2)
BACKWARD = (4, 2, 2)
ANY = pl.BlockSpec(memory_space=pl.ANY)
SMEM = pl.BlockSpec(memory_space=pltpu.SMEM)
VMEM = pl.BlockSpec(memory_space=pltpu.VMEM)
HBM = pl.BlockSpec(memory_space=pltpu.HBM)


def spans(parts, size):
    total, at, out = sum(parts), 0, []
    for part in parts:
        out.append((at * size // total, part * size // total))
        at += part
    return out


def high(value, count):
    return value >> (count.bit_length() - 1) if count & (count - 1) == 0 else value // count


def low(value, count):
    return value & (count - 1) if count & (count - 1) == 0 else value % count


def column_slots(owner, me, mp, group):
    distances = [high(owner[me * mp + c], mp) ^ me for c in range(mp)]
    return [
        k * group + sum([(other == k).astype(jnp.int32) for other in distances[:c]], jnp.int32(0))
        for c, k in enumerate(distances)
    ]


def list_slots(owner, slots, me, dp, mp, group):
    owners = [owner[b] for b in range(dp * mp)]
    found = []
    for band in range(dp):
        last = [jnp.int32(0)] * group
        for o in owners[band * mp : (band + 1) * mp]:
            match = high(o, mp) == me
            last = [jnp.where(match, new, old) for new, old in zip(last[1:] + [low(o, mp)], last)]
        found.append(last)
    for band in range(dp):
        for rank, m in enumerate(found[band]):
            slots[m] = (band ^ me) * group + rank


def call(body, outs, inputs, table, scratch=(), ins=VMEM, out=VMEM, aliases=None, flops=0, mib=8):
    ins = ins if isinstance(ins, list) else [ins] * len(inputs)
    out = out if isinstance(out, list) else [out] * len(outs)
    return pl.pallas_call(
        body,
        out_shape=outs,
        in_specs=[SMEM] + ins,
        out_specs=out,
        scratch_shapes=list(scratch),
        input_output_aliases=aliases or {},
        cost_estimate=pl.CostEstimate(flops=flops, bytes_accessed=1 << 21, transcendentals=0),
        compiler_params=pltpu.CompilerParams(vmem_limit_bytes=mib << 20),
    )(table, *inputs)


def pack_first(grad, owner, dp, mp, blk, cut):
    rows = grad.shape[0]
    group = mp // dp
    at, width = cut

    def body(grad, owner_ref, *rest):
        outs, (plan, owner, buf, sems) = rest[:dp], rest[dp:]
        table = pltpu.make_async_copy(owner_ref, owner, sems.at[mp])
        table.start()
        copies = [
            pltpu.make_async_copy(grad.at[:, pl.ds(c * blk + at, width)], buf.at[c], sems.at[c])
            for c in range(mp)
        ]
        for copy in copies:
            copy.start()
        table.wait()
        slots = column_slots(owner, lax.axis_index("dp"), mp, group)
        for c, slot in enumerate(slots):
            plan[slot] = c
        for c, slot in enumerate(slots):
            copies[c].wait()
            for k in range(dp):

                @pl.when(high(slot, group) == k)
                def _(k=k, c=c, slot=slot):
                    outs[k][low(slot, group)] = buf[c]

    outs = [jax.ShapeDtypeStruct((group, rows, width), grad.dtype)] * dp
    outs.append(jax.ShapeDtypeStruct((mp,), jnp.int32))
    flat = pl.pallas_call(
        body,
        out_shape=outs,
        in_specs=[HBM, HBM],
        out_specs=[VMEM] * dp + [SMEM],
        scratch_shapes=[
            pltpu.SMEM(owner.shape, jnp.int32),
            pltpu.VMEM((mp, rows, width), grad.dtype),
            pltpu.SemaphoreType.DMA((mp + 1,)),
        ],
        cost_estimate=pl.CostEstimate(flops=0, bytes_accessed=1 << 21, transcendentals=0),
        compiler_params=pltpu.CompilerParams(vmem_limit_bytes=8 << 20),
        name="pack0",
    )(
        pltpu.with_memory_space_constraint(grad, pltpu.HBM),
        pltpu.with_memory_space_constraint(owner, pltpu.HBM),
    )
    return flat[:dp], flat[dp]


def pack(grad, plan, owner, dp, mp, blk, cut):
    rows = grad.shape[0]
    group = mp // dp
    at, width = cut

    def body(plan, grad, *rest):
        rest = list(rest)
        owner_ref = None if owner is None else rest.pop(0)
        outs, sems = rest[:dp], rest[-1]
        copies = []
        for k in list(range(1, dp)) + [0]:
            for j in range(group):
                start = pl.multiple_of(plan[k * group + j] * blk + at, 128)
                copy = pltpu.make_async_copy(
                    grad.at[:, pl.ds(start, width)], outs[k].at[j], sems.at[k * group + j]
                )
                copy.start()
                copies.append(copy)
        if owner is not None:
            list_slots(owner_ref, rest[dp], lax.axis_index("dp"), dp, mp, group)
        for copy in copies:
            copy.wait()

    outs = [jax.ShapeDtypeStruct((group, rows, width), grad.dtype)] * dp
    out, inputs, ins = [VMEM] * dp, [pltpu.with_memory_space_constraint(grad, pltpu.HBM)], [HBM]
    if owner is not None:
        outs.append(jax.ShapeDtypeStruct((mp,), jnp.int32))
        out, inputs, ins = out + [SMEM], inputs + [owner], ins + [SMEM]
    flat = call(body, outs, inputs, plan, [pltpu.SemaphoreType.DMA((mp,))], ins=ins, out=out)
    return flat[:dp], flat[dp:]


def square_sum(grad, plan):
    rows, cols = grad.shape
    step = min(1024, cols)

    def body(plan, grad, out):
        total = jnp.zeros((8, step), jnp.float32)
        for i in range(cols // step):
            values = grad[:, i * step : (i + 1) * step].astype(jnp.float32)
            total = total + jnp.sum((values * values).reshape(rows // 8, 8, step), axis=0)
        out[...] = jnp.full(out.shape, jnp.sum(total), jnp.float32)

    return call(body, [jax.ShapeDtypeStruct((8, 128), jnp.float32)], [grad], plan)[0]


def route(got, plan, dp, mp):
    group, rows, width = got[0].shape

    def body(plan, *rest):
        got, outs = rest[:dp], rest[dp:]
        mine = lax.axis_index("mp")
        for kk in range(mp):
            entry = plan[mine ^ kk]
            for k in range(dp):

                @pl.when(high(entry, group) == k)
                def _(k=k, kk=kk, entry=entry):
                    outs[kk][...] = got[k][low(entry, group)]

    outs = [jax.ShapeDtypeStruct((rows, width), got[0].dtype)] * mp
    return call(body, outs, got, plan)


def unroute(pieces, plan, dp, mp):
    rows, width = pieces[0].shape
    group = mp // dp

    def body(plan, *rest):
        pieces, outs = rest[:mp], rest[mp:]
        mine = lax.axis_index("mp")
        for kk in range(mp):
            entry = plan[mine ^ kk]
            for k in range(dp):

                @pl.when(high(entry, group) == k)
                def _(k=k, kk=kk, entry=entry):
                    outs[k][low(entry, group)] = pieces[kk][...]

    outs = [jax.ShapeDtypeStruct((group, rows, width), pieces[0].dtype)] * dp
    return call(body, outs, list(pieces), plan)


def place(parts, old, plan, dp, mp, blk, cuts):
    group, rows = parts[0][0].shape[:2]
    count = len(cuts)

    def body(plan, *rest):
        parts, out, sems = rest[: count * dp], rest[-2], rest[-1]
        copies = []
        for k in range(dp):
            for j in range(group):
                for c, (at, width) in enumerate(cuts):
                    start = pl.multiple_of(plan[k * group + j] * blk + at, 128)
                    copy = pltpu.make_async_copy(
                        parts[c * dp + k].at[j],
                        out.at[:, pl.ds(start, width)],
                        sems.at[(c * dp + k) * group + j],
                    )
                    copy.start()
                    copies.append(copy)
        for copy in copies:
            copy.wait()

    outs = [jax.ShapeDtypeStruct((rows, mp * blk), parts[0][0].dtype)]
    inputs = [part for chunk in parts for part in chunk]
    ins = [VMEM] * len(inputs)
    aliases = None
    if old is not None:
        aliases = {1 + len(inputs): 0}
        inputs, ins = inputs + [old], ins + [ANY]
    scratch = [pltpu.SemaphoreType.DMA((mp * count,))]
    return call(body, outs, inputs, plan, scratch, ins, ANY, aliases)[0]


def gather(pieces, block, mp, at, width):
    rows = pieces[0].shape[0]
    mine = lax.axis_index("mp")
    for kk in range(mp):
        start = pl.multiple_of((mine ^ kk) * rows, 16)
        block[pl.ds(start, rows), at : at + width] = pieces[kk][...]


def partial_update(pieces, left_root, right_root, old, plan, mp, at, width):
    blk = left_root.shape[0]
    tile = min(512, blk)

    def body(plan, *rest):
        pieces = rest[:mp]
        left, right = rest[mp : mp + 2]
        block, total = rest[-2:]
        gather(pieces, block, mp, at, width)

        @pl.loop(0, blk // tile, unroll=True)
        def _(i):
            span = pl.ds(pl.multiple_of(i * tile, tile), tile)
            half = jnp.dot(left[span, :], block[:, at : at + width], preferred_element_type=jnp.float32)
            term = jnp.dot(
                half.astype(block.dtype), right[at : at + width, :], preferred_element_type=jnp.float32
            )
            total[span, :] = term if old is None else total[span, :] + term

    outs = [
        jax.ShapeDtypeStruct((blk, blk), pieces[0].dtype),
        jax.ShapeDtypeStruct((blk, blk), jnp.float32),
    ]
    inputs = [*pieces, left_root, right_root, *(old or ())]
    aliases = None if old is None else {mp + 3: 0, mp + 4: 1}
    return call(body, outs, inputs, plan, aliases=aliases, flops=4 * blk * blk * width, mib=24)


def deal(update, outs, rows, mp, cuts):
    mine = lax.axis_index("mp")
    for c, (start, size) in enumerate(cuts):
        for kk in range(mp):
            row = pl.multiple_of((mine ^ kk) * rows, 16)
            outs[c * mp + kk][...] = update[pl.ds(row, rows), start : start + size]


def last_update(pieces, left_root, right_root, block, total, scale, plan, mp, at, width, cut):
    rows = pieces[0].shape[0]
    blk = left_root.shape[0]
    tile = blk
    start, size = cut

    def body(plan, *rest):
        pieces = rest[:mp]
        left, right, total, scale, _, block, half = rest[mp : mp + 7]
        outs, update = rest[mp + 7 : -1], rest[-1]
        gather(pieces, block, mp, at, width)
        scaling = scale[0:1, 0:1]

        @pl.loop(0, blk // tile, unroll=True)
        def _(i):
            span = pl.ds(pl.multiple_of(i * tile, tile), tile)
            term = jnp.dot(left[span, :], block[:, at : at + width], preferred_element_type=jnp.float32)
            half[span, :] = term.astype(half.dtype)
            term = jnp.dot(
                term.astype(half.dtype),
                right[at : at + width, start : start + size],
                preferred_element_type=jnp.float32,
            )
            update[span, :] = ((total[span, start : start + size] + term) * scaling).astype(update.dtype)

        deal(update, outs, rows, mp, [(0, size)])

    dtype = pieces[0].dtype
    outs = [jax.ShapeDtypeStruct((blk, blk), dtype), jax.ShapeDtypeStruct((blk, width), dtype)]
    outs += [jax.ShapeDtypeStruct((rows, size), dtype)] * mp
    scratch = [pltpu.VMEM((blk, size), dtype)]
    inputs = [*pieces, left_root, right_root, total, scale, block]
    flops = 2 * blk * width * (blk + size)
    flat = call(body, outs, inputs, plan, scratch, aliases={mp + 5: 0}, flops=flops, mib=24)
    return flat[0], flat[1], flat[2:]


def rest_update(half, right_root, total, scale, rows, plan, mp, at, cuts):
    blk, width = half.shape
    tile = min(512, blk)
    base = cuts[0][0]

    def body(plan, half, right, total, scale, *rest):
        outs, update = rest[:-1], rest[-1]
        scaling = scale[0:1, 0:1]

        @pl.loop(0, blk // tile, unroll=True)
        def _(i):
            span = pl.ds(pl.multiple_of(i * tile, tile), tile)
            term = jnp.dot(half[span, :], right[at : at + width, base:], preferred_element_type=jnp.float32)
            update[span, :] = ((total[span, base:] + term) * scaling).astype(update.dtype)

        deal(update, outs, rows, mp, [(start - base, size) for start, size in cuts])

    outs = [jax.ShapeDtypeStruct((rows, size), half.dtype) for _, size in cuts for _ in range(mp)]
    scratch = [pltpu.VMEM((blk, blk - base), half.dtype)]
    flops = 2 * blk * width * (blk - base)
    flat = call(body, outs, [half, right_root, total, scale], plan, scratch, flops=flops, mib=24)
    return [flat[c * mp : (c + 1) * mp] for c in range(len(cuts))]


def swap(value, axis, distance):
    count = lax.axis_size(axis)
    return lax.ppermute(value, axis, [(i, i ^ distance) for i in range(count)])


def per_device(grad, owner, left_stat, right_stat, left_root, right_root):
    dp, mp = lax.axis_size("dp"), lax.axis_size("mp")
    blk = left_root.shape[-1]
    left_root, right_root = left_root[0], right_root[0]
    forward, backward = spans(FORWARD, blk), spans(BACKWARD, blk)

    chunk, plan = pack_first(grad, owner, dp, mp, blk, forward[0])
    packed, slots = [chunk], None
    for c, cut in enumerate(forward[1:], 1):
        chunk, found = pack(grad, plan, owner if slots is None else None, dp, mp, blk, cut)
        packed.append(chunk)
        slots = found[0] if found else slots
    crossed = [[part if k == 0 else swap(part, "dp", k) for k, part in enumerate(chunk)] for chunk in packed]
    total = square_sum(grad, plan)
    total = total + swap(total, "mp", 1)
    terms = [swap(total, "mp", k) for k in range(2, mp, 2)]
    total = sum(terms, total)
    terms = [swap(total, "dp", k) for k in range(1, dp)]
    total = sum(terms, total)
    mean_square = total / (grad.size * dp * mp)
    scale = clip_level / jnp.sqrt(mean_square + 1e-06)
    factor = (1.0 - beta_stat) * scale * scale / blk

    arrived = []
    for c in range(len(forward)):
        pieces = route(crossed[c], slots, dp, mp)
        moved = list(pieces)
        for k in range(1, mp):
            moved[k] = swap(pieces[k], "mp", k)
        arrived.append(moved)

    state = None
    for c, (at, width) in enumerate(forward[:-1]):
        state = partial_update(arrived[c], left_root, right_root, state, plan, mp, at, width)
    at, width = forward[-1]
    rows = arrived[0][0].shape[0]
    block, half, first = last_update(
        arrived[-1], left_root, right_root, *state, scale, plan, mp, at, width, backward[0]
    )
    leaving = [first] + rest_update(half, right_root, state[1], scale, rows, plan, mp, at, backward[1:])

    parts = []
    for c in range(len(backward)):
        pieces = list(leaving[c])
        for k in range(1, mp):
            pieces[k] = swap(leaving[c][k], "mp", k)
        chunk = list(unroute(pieces, slots, dp, mp))
        for k in range(1, dp):
            chunk[k] = swap(chunk[k], "dp", k)
        parts.append(chunk)
    out = place(parts[:-1], None, plan, dp, mp, blk, backward[:-1])
    out = place(parts[-1:], out, plan, dp, mp, blk, backward[-1:])

    factor = factor[0, 0]
    left_gram = jnp.dot(block, block.T, preferred_element_type=jnp.float32)
    left_new = beta_stat * left_stat[0] + factor * left_gram
    right_gram = jnp.dot(block.T, block, preferred_element_type=jnp.float32)
    right_new = beta_stat * right_stat[0] + factor * right_gram
    return (left_new[None], right_new[None], out)


def solution(mesh):
    split = P(("dp", "mp"), None, None)
    rows = P(("dp", "mp"), None)

    return jax.shard_map(
        per_device,
        mesh=mesh,
        in_specs=(rows, P(), split, split, split, split),
        out_specs=(split, split, rows),
        check_vma=False,
    )
```
